128 devices in a mesh: grp: 4 (over x), seq: 32 (over y, z, core).
Axes of the slice: x: 4, y: 4, z: 4, core: 2. Of those that a mesh axis runs over, the one named last changes fastest.
Arguments:
- lin_q: bfloat16 [8192, 8192], P('seq', 'grp'), may hold values from -6 to 6
- lin_k: bfloat16 [8192, 8192], P('seq', 'grp'), may hold values from -6 to 6
- lin_v: bfloat16 [8192, 8192], P('seq', 'grp'), may hold values from -60 to 60
- lin_gain: float32 [8192], P('grp'), may hold values from 0.1 to 1.9
- soft_q: bfloat16 [8192, 8192], P('seq', 'grp'), may hold values from -6 to 6
- soft_k: bfloat16 [8192, 8192], P('seq', 'grp'), may hold values from -12.5 to 12.5
- soft_v: bfloat16 [8192, 8192], P('seq', 'grp'), may hold values from -6 to 6
Outputs:
- lin_out: bfloat16 [8192, 8192], P('seq', 'grp')
- soft_out: bfloat16 [8192, 8192], P('seq', 'grp')
The draws below stay inside these ranges and needn't reach their ends.
All inputs are finite; a program needn't handle non-finite values.
Results may differ from the reference program's by a relative error of at most 0.0031.
Values may be sent and summed in bfloat16 or wider, within the bound.
A program may use at most 192 MiB of HBM per device.

```python
import jax
import jax.numpy as jnp
from jax import lax

HEADS = 64
HEAD_DIM = 128
TOK_DEV = 256
SEQ_LEN = 8192
WIDTH = 8192
N_SEQ = 32


def soft_pair(key):
    base_key = jax.random.fold_in(key, 7)
    key_query, key_keys = jax.random.split(base_key, 2)
    seq_len = TOK_DEV * N_SEQ
    full_width = HEADS * HEAD_DIM
    shape_full = (seq_len, full_width)
    queries = jnp.clip(jax.random.normal(key_query, shape_full, jnp.float32), -6.0, 6.0)
    keys_all = 2.5 * jnp.clip(jax.random.normal(key_keys, shape_full, jnp.float32), -5.0, 5.0)
    return (queries, keys_all)


def draw_soft_q(key, part):
    return soft_pair(key)[0].astype(jnp.bfloat16)


def draw_soft_k(key, part):
    return soft_pair(key)[1].astype(jnp.bfloat16)


def draw_lin_v(key, part):
    seq_len = TOK_DEV * N_SEQ
    full_width = HEADS * HEAD_DIM
    value_key = jax.random.fold_in(key, 11)
    levels = (jnp.arange(full_width) // HEAD_DIM).astype(jnp.float32) / (HEADS - 1)
    base_draw = jnp.clip(jax.random.normal(value_key, (seq_len, full_width), jnp.float32), -6.0, 6.0)
    column_scale = jnp.power(10.0, levels)
    return (base_draw * column_scale[None, :]).astype(jnp.bfloat16)


def shard_levels(own_key, shape, shards, smallest, high):
    level, own = 1.0, jax.random.fold_in(own_key, 6)
    for axis_at, blocks in shards:
        heights = jnp.exp(jax.random.uniform(jax.random.fold_in(own, axis_at), (blocks,), jnp.float32, smallest / len(shards), high / len(shards)))
        level = level * jnp.repeat(heights, shape[axis_at] // blocks).reshape([-1 if axis == axis_at else 1 for axis in range(len(shape))])
    return level


def centred(rng, shape, deviation, bound, shards=(), kind=jnp.bfloat16):
    loudness = shard_levels(rng, shape, shards, -0.22, 0.18) if shards else 1.0
    result = jax.random.normal(rng, shape, jnp.float32) * deviation * loudness
    return jnp.minimum(jnp.maximum(result, -bound), bound).astype(kind)


def setup_inputs(seed: int = 0) -> dict:
    key_of = jax.random.split(jax.random.key(seed), 8)
    lin_q = centred(key_of[0], (SEQ_LEN, WIDTH), 1.0, 6.0, ((0, 32), (1, 4)))
    lin_k = centred(key_of[1], (SEQ_LEN, WIDTH), 1.0, 6.0, ((0, 32), (1, 4)))
    lin_v = draw_lin_v(jax.random.fold_in(key_of[7], 71), 0)
    lin_gain = jnp.clip(1.0 + 0.18 * jax.random.normal(key_of[3], (WIDTH,), jnp.float32), 0.1, 1.9)
    soft_q = draw_soft_q(jax.random.fold_in(key_of[7], 71), 0)
    soft_k = draw_soft_k(jax.random.fold_in(key_of[7], 71), 0)
    soft_v = centred(key_of[6], (SEQ_LEN, WIDTH), 1.0, 6.0, ((0, 32), (1, 4)))
    return dict(lin_q=lin_q, lin_k=lin_k, lin_v=lin_v, lin_gain=lin_gain, soft_q=soft_q, soft_k=soft_k, soft_v=soft_v)


highest = lax.Precision.HIGHEST
epsilon = 1e-06

def reference(lin_q, lin_k, lin_v, lin_gain, soft_q, soft_k, soft_v):
    seq_len = TOK_DEV * N_SEQ
    full_width = HEADS * HEAD_DIM

    def split_blocks(source):
        return source.astype(jnp.float32).reshape(N_SEQ, TOK_DEV, HEADS, HEAD_DIM)
    causal = jnp.tril(jnp.ones((TOK_DEV, TOK_DEV), jnp.float32))

    def block_step(memory, inputs):
        queries, keys_block, values = inputs
        carried = jnp.einsum('thd,hde->the', queries, memory, precision=highest)
        scores = jnp.einsum('thd,shd->hts', queries, keys_block, precision=highest) * causal[None]
        within = jnp.einsum('hts,she->the', scores, values, precision=highest)
        own_state = jnp.einsum('thd,the->hde', keys_block, values, precision=highest)
        return (memory + own_state, within + carried)
    initial = jnp.zeros((HEADS, HEAD_DIM, HEAD_DIM), jnp.float32)
    final_state, mixed_out = lax.scan(block_step, initial, (split_blocks(lin_q), split_blocks(lin_k), split_blocks(lin_v)))
    mixed_out = mixed_out.reshape(seq_len, full_width)
    squares = lax.optimization_barrier(jnp.sum(mixed_out * mixed_out, axis=1))
    inverse = lax.rsqrt(squares / full_width + epsilon)
    lin_out = (mixed_out * inverse[:, None] * lin_gain).astype(jnp.bfloat16)
    scale = HEAD_DIM ** (-0.5)

    def one_head(operands):
        head_q, head_k, head_v = operands
        block_rows = min(512, seq_len)
        pieces = []
        for block_index in range(seq_len // block_rows):
            first_row = block_index * block_rows
            last_row = first_row + block_rows
            scores = jnp.dot(head_q[first_row:last_row], head_k[:last_row].T, preferred_element_type=jnp.float32) * scale
            positions_q = first_row + jnp.arange(block_rows)[:, None]
            positions_k = jnp.arange(last_row)[None, :]
            scores = jnp.where(positions_k <= positions_q, scores, -1e+30)
            largest = lax.optimization_barrier(jnp.max(scores, axis=1, keepdims=True))
            exponent = jnp.exp(scores - largest)
            denominator = lax.optimization_barrier(jnp.sum(exponent, axis=1, keepdims=True))
            weights = exponent.astype(jnp.bfloat16)
            numerator = jnp.dot(weights, head_v[:last_row], preferred_element_type=jnp.float32)
            pieces.append((numerator / denominator).astype(jnp.bfloat16))
        return jnp.concatenate(pieces, axis=0)

    def by_heads(source):
        return source.reshape(seq_len, HEADS, HEAD_DIM).transpose(1, 0, 2)
    heads_out = lax.map(one_head, (by_heads(soft_q), by_heads(soft_k), by_heads(soft_v)))
    soft_out = heads_out.transpose(1, 0, 2).reshape(seq_len, full_width)
    return (lin_out, soft_out)
```

```python
import functools

import jax
import jax.numpy as jnp
from jax import lax
from jax.experimental import pallas as pl
from jax.experimental.pallas import tpu as pltpu
from jax.sharding import PartitionSpec as P

HEADS = 64
HEAD_DIM = 128
EPSILON = 1e-06
MESH = pl.DeviceIdType.MESH
F32 = jnp.float32
BF16 = jnp.bfloat16

CHIPS = 16
SIDE = 4
ROWS = 256
SEQ = 8192
CHUNK = 1024
SCALE = HEAD_DIM ** -0.5
LOG2E = 1.4426950408889634


def kernel(
    lin_q, lin_k, lin_v, gain, soft_q, soft_k, soft_v,
    lin_out, soft_out,
    lq, lk, lv, mixed, state, half_in, chip_half, gathered, prefix_half, half_out, half_got,
    squares, kbuf, vbuf, qbuf, obuf, sbuf, pbuf, lbuf, mbuf,
    load_sem, k_send, k_recv, k_fwd, v_send, v_recv, v_fwd, q_send, q_recv, o_send, o_recv,
    x_sem, one_send, one_recv, two_send, two_recv, sq_send, sq_recv,
):
    me = lax.axis_index("seq")
    grp = lax.axis_index("grp")
    chip, core = me // 2, me % 2
    partner = chip * 2 + 1 - core
    y, z = chip // SIDE, chip % SIDE

    def chip_to(i):
        return (y + i // SIDE + i) % SIDE * SIDE + (z + i) % SIDE

    def chip_from(i):
        return (y + 2 * SIDE * SIDE - i // SIDE - i) % SIDE * SIDE + (z + SIDE * SIDE - i) % SIDE

    def cols(h):
        return pl.ds(pl.multiple_of(h * HEAD_DIM, HEAD_DIM), HEAD_DIM)

    def remote(src, dst, send, recv, seq):
        return pltpu.make_async_remote_copy(
            src_ref=src, dst_ref=dst, send_sem=send, recv_sem=recv,
            device_id={"seq": seq}, device_id_type=MESH)

    def arrived(dst, sem):
        pltpu.make_async_copy(dst, dst, sem).wait()

    loads = [pltpu.make_async_copy(src, dst, load_sem.at[n])
             for n, (src, dst) in enumerate(((lin_q, lq), (lin_k, lk), (lin_v, lv)))]
    for load in loads:
        load.start()

    barrier = pltpu.get_barrier_semaphore()

    @pl.loop(1, 2 * CHIPS)
    def _(i):
        pl.semaphore_signal(barrier, inc=1, device_id={"seq": lax.rem(me + i, 2 * CHIPS)}, device_id_type=MESH)

    for i in range(1, 4):
        pl.semaphore_signal(barrier, inc=1, device_id={"grp": lax.rem(grp + i, 4)}, device_id_type=MESH)

    for load in loads:
        load.wait()

    @pl.loop(0, CHIPS)
    def _(h):
        keys, values = lk[:, cols(h)], lv[:, cols(h)]
        state[h] = lax.dot_general(keys, values, (((0,), (0,)), ((), ())), preferred_element_type=F32)
        scores = lax.dot_general(lq[:, cols(h)], keys, (((1,), (1,)), ((), ())), preferred_element_type=F32)
        row = lax.broadcasted_iota(jnp.int32, (ROWS, ROWS), 0)
        col = lax.broadcasted_iota(jnp.int32, (ROWS, ROWS), 1)
        scores = jnp.where(col <= row, scores, 0.0)
        high = scores.astype(BF16)
        low = (scores - high.astype(F32)).astype(BF16)
        mixed[:, cols(h)] = (jnp.dot(high, values, preferred_element_type=F32)
                             + jnp.dot(low, values, preferred_element_type=F32))

    pl.semaphore_wait(barrier, 2 * CHIPS - 1 + 3)

    away = pl.ds(pl.multiple_of((1 - core) * 64, 64), 64)
    home = pl.ds(pl.multiple_of(core * 64, 64), 64)
    swap = remote(state.at[:, away, :], half_in, x_sem.at[0], x_sem.at[1], partner)
    swap.start()

    def spread(src, buf, send, recv, fwd):
        pltpu.make_async_copy(src.at[:, cols(chip)], buf.at[me], recv.at[me]).start()
        remote(src.at[:, cols(chip)], buf.at[me], fwd.at[0], recv.at[me], partner).start()

        @pl.loop(1, CHIPS)
        def _(i):
            c = chip_to(i)
            remote(src.at[:, cols(c)], buf.at[me], send.at[i], recv.at[me], 2 * c + core).start()

    def forward(buf, recv, fwd):
        @pl.loop(1, CHIPS)
        def _(i):
            s = 2 * chip_from(i) + core
            arrived(buf.at[s], recv.at[s])
            remote(buf.at[s], buf.at[s], fwd.at[i], recv.at[s], partner).start()

        arrived(buf.at[me], recv.at[me])

        @pl.loop(0, CHIPS)
        def _(i):
            s = 2 * chip_from(i) + 1 - core
            arrived(buf.at[s], recv.at[s])

    def sent(buf, src, send, fwd):
        remote(src.at[:, cols(chip)], buf.at[me], fwd.at[0], fwd.at[0], partner).wait_send()

        @pl.loop(1, CHIPS)
        def _(i):
            remote(src.at[:, cols(0)], buf.at[me], send.at[i], send.at[i], partner).wait_send()
            remote(buf.at[me], buf.at[me], fwd.at[i], fwd.at[i], partner).wait_send()

    spread(soft_k, kbuf, k_send, k_recv, k_fwd)

    q_core = (core + chip) % 2

    @pl.when(q_core == core)
    def _():
        pltpu.make_async_copy(soft_q.at[:, cols(chip)], qbuf.at[chip], q_recv.at[chip]).start()

    @pl.when(q_core != core)
    def _():
        remote(soft_q.at[:, cols(chip)], qbuf.at[chip], q_send.at[0], q_recv.at[chip], partner).start()

    @pl.loop(1, CHIPS)
    def _(i):
        c = chip_to(i)
        remote(soft_q.at[:, cols(c)], qbuf.at[chip], q_send.at[i], q_recv.at[chip], 2 * c + q_core).start()

    swap.wait()

    @pl.loop(0, CHIPS)
    def _(h):
        total = state[h, home, :] + half_in[h]
        chip_half[h] = total

        @pl.when(h == chip)
        def _():
            gathered[h] = total

    @pl.loop(1, CHIPS)
    def _(i):
        c = chip_to(i)
        remote(chip_half.at[c], gathered.at[chip], one_send.at[i], one_recv.at[chip], 2 * c + core).start()

    spread(soft_v, vbuf, v_send, v_recv, v_fwd)
    forward(kbuf, k_recv, k_fwd)

    def position(b):
        return 2 * b + (b + core) % 2

    def first_chunk(b):
        pair = b // 2
        return pair * (pair + 1) + b % 2 * (pair + 1)

    @pl.loop(0, CHIPS)
    def _(i):
        b = chip_from(i)
        s = position(b)
        chunks = b // 2 + 1
        base = first_chunk(b)
        arrived(qbuf.at[b], q_recv.at[b])
        queries = qbuf[b]
        mbuf[...] = jnp.full((ROWS, 128), -1e30, F32)

        def score(t, last):
            keys = kbuf[pl.ds(t * 4, 4)].reshape(CHUNK, HEAD_DIM)
            value = lax.dot_general(queries, keys, (((1,), (1,)), ((), ())), preferred_element_type=F32)
            if last:
                row = lax.broadcasted_iota(jnp.int32, (ROWS, CHUNK), 0) + s * ROWS
                col = lax.broadcasted_iota(jnp.int32, (ROWS, CHUNK), 1) + t * CHUNK
                value = jnp.where(col <= row, value, -1e30)
            sbuf[t] = value
            top = mbuf[...]
            for n in range(CHUNK // 128):
                top = jnp.maximum(top, value[:, n * 128:(n + 1) * 128])
            mbuf[...] = top

        @pl.loop(0, chunks - 1)
        def _(t):
            score(t, False)

        score(chunks - 1, True)
        top = jnp.max(mbuf[...], axis=1, keepdims=True) * (SCALE * LOG2E)
        mbuf[...] = jnp.broadcast_to(top, (ROWS, 128))
        lbuf[b] = jnp.zeros((ROWS, 128), F32)

        @pl.loop(0, chunks)
        def _(t):
            top = mbuf[...]
            total = lbuf[b]
            for n in range(CHUNK // 128):
                part = slice(n * 128, (n + 1) * 128)
                expo = jnp.exp2(sbuf[t, :, part] * (SCALE * LOG2E) - top)
                total = total + expo
                pbuf[base + t, :, part] = expo.astype(BF16)
            lbuf[b] = total

        @pl.when(i == 8)
        def _():
            def running(c, total):
                @pl.when(c != chip)
                def _():
                    arrived(gathered.at[c], one_recv.at[c])

                own = gathered[c]
                gathered[c] = total

                @pl.when(c == chip)
                def _():
                    prefix_half[c] = total

                return total + own

            lax.fori_loop(0, CHIPS, running, jnp.zeros((64, HEAD_DIM), F32))

            @pl.loop(1, CHIPS)
            def _(i):
                c = chip_to(i)
                remote(gathered.at[c], prefix_half.at[chip], two_send.at[i], two_recv.at[chip], 2 * c + core).start()

        @pl.when(i == 12)
        def _():
            forward(vbuf, v_recv, v_fwd)

    @pl.loop(0, CHIPS)
    def _(i):
        b = chip_from(i)
        s = position(b)
        chunks = b // 2 + 1
        base = first_chunk(b)

        def step(t, acc):
            values = vbuf[pl.ds(t * 4, 4)].reshape(CHUNK, HEAD_DIM)
            return acc + jnp.dot(pbuf[base + t], values, preferred_element_type=F32)

        acc = lax.fori_loop(0, chunks, step, jnp.zeros((ROWS, HEAD_DIM), F32))
        obuf[b] = (acc / jnp.sum(lbuf[b], axis=1, keepdims=True)).astype(BF16)

        @pl.when(s == me)
        def _():
            pltpu.make_async_copy(obuf.at[b], soft_out.at[:, cols(chip)], o_recv.at[chip]).start()

        @pl.when(s != me)
        def _():
            remote(obuf.at[b], soft_out.at[:, cols(chip)], o_send.at[b], o_recv.at[chip], s).start()

    @pl.loop(0, CHIPS)
    def _(h):
        @pl.when(h != chip)
        def _():
            arrived(prefix_half.at[h], two_recv.at[h])

    first = jnp.where(core == 0, 1.0, 0.0).astype(F32)
    half_out[...] = prefix_half[...] + first * state[:, 0:64, :]
    swap_two = remote(half_out, half_got, x_sem.at[2], x_sem.at[3], partner)
    swap_two.start()
    state[:, home, :] = prefix_half[...] + (1.0 - first) * half_in[...]
    swap_two.wait()
    state[:, away, :] = half_got[...]
    squares[0] = jnp.zeros((ROWS, 128), F32)

    @pl.loop(0, CHIPS)
    def _(h):
        full = state[h]
        high = full.astype(BF16)
        low = (full - high.astype(F32)).astype(BF16)
        queries = lq[:, cols(h)]
        out = (mixed[:, cols(h)] + jnp.dot(queries, high, preferred_element_type=F32)
               + jnp.dot(queries, low, preferred_element_type=F32))
        mixed[:, cols(h)] = out
        squares[0] += out * out

    swaps = []
    for i in range(1, 4):
        copy = pltpu.make_async_remote_copy(
            src_ref=squares.at[0], dst_ref=squares.at[i], send_sem=sq_send.at[i], recv_sem=sq_recv.at[i],
            device_id={"grp": lax.rem(grp + i, 4)}, device_id_type=MESH)
        copy.start()
        swaps.append(copy)
    for copy in swaps:
        copy.wait()
    total = squares[0] + squares[1] + squares[2] + squares[3]
    inverse = lax.rsqrt(jnp.sum(total, axis=1, keepdims=True) / (HEADS * HEAD_DIM) + EPSILON)
    mbuf[...] = jnp.broadcast_to(inverse, (ROWS, 128))

    @pl.loop(0, CHIPS)
    def _(h):
        lk[:, cols(h)] = (mixed[:, cols(h)] * mbuf[...] * gain[:, cols(h)]).astype(BF16)

    store = pltpu.make_async_copy(lk, lin_out, load_sem.at[3])
    store.start()

    sent(kbuf, soft_k, k_send, k_fwd)
    sent(vbuf, soft_v, v_send, v_fwd)

    @pl.when(q_core != core)
    def _():
        remote(soft_q.at[:, cols(0)], qbuf.at[0], q_send.at[0], q_send.at[0], partner).wait_send()

    @pl.loop(1, CHIPS)
    def _(i):
        remote(soft_q.at[:, cols(0)], qbuf.at[0], q_send.at[i], q_send.at[i], partner).wait_send()
        remote(chip_half.at[0], chip_half.at[0], one_send.at[i], one_send.at[i], partner).wait_send()
        remote(chip_half.at[0], chip_half.at[0], two_send.at[i], two_send.at[i], partner).wait_send()

    @pl.loop(0, CHIPS)
    def _(b):
        @pl.when(position(b) != me)
        def _():
            remote(obuf.at[0], obuf.at[0], o_send.at[b], o_send.at[b], partner).wait_send()

        arrived(soft_out.at[:, cols(b)], o_recv.at[b])

    store.wait()


def shards(lin_q, lin_k, lin_v, lin_gain, soft_q, soft_k, soft_v):
    half = pltpu.VMEM((CHIPS, 64, HEAD_DIM), F32)
    tokens = pltpu.VMEM((ROWS, CHIPS * HEAD_DIM), BF16)
    dma = pltpu.SemaphoreType.DMA
    hbm = pl.BlockSpec(memory_space=pl.ANY)
    shape = jax.ShapeDtypeStruct(lin_q.shape, BF16)
    return pl.pallas_call(
        kernel,
        out_shape=(shape, shape),
        in_specs=[hbm, hbm, hbm, pl.BlockSpec(memory_space=pltpu.VMEM), hbm, hbm, hbm],
        out_specs=(hbm, hbm),
        scratch_shapes=[
            tokens, tokens, tokens,
            pltpu.VMEM((ROWS, CHIPS * HEAD_DIM), F32),
            pltpu.VMEM((CHIPS, HEAD_DIM, HEAD_DIM), F32),
            half, half, half, half, half, half,
            pltpu.VMEM((4, ROWS, 128), F32),
            pltpu.VMEM((2 * CHIPS, ROWS, HEAD_DIM), BF16),
            pltpu.VMEM((2 * CHIPS, ROWS, HEAD_DIM), BF16),
            pltpu.VMEM((CHIPS, ROWS, HEAD_DIM), BF16),
            pltpu.VMEM((CHIPS, ROWS, HEAD_DIM), BF16),
            pltpu.VMEM((SEQ // CHUNK, ROWS, CHUNK), F32),
            pltpu.VMEM((72, ROWS, CHUNK), BF16),
            pltpu.VMEM((CHIPS, ROWS, 128), F32),
            pltpu.VMEM((ROWS, 128), F32),
            dma((4,)),
            dma((CHIPS,)), dma((2 * CHIPS,)), dma((CHIPS,)),
            dma((CHIPS,)), dma((2 * CHIPS,)), dma((CHIPS,)),
            dma((CHIPS,)), dma((CHIPS,)),
            dma((CHIPS,)), dma((CHIPS,)),
            dma((4,)),
            dma((CHIPS,)), dma((CHIPS,)),
            dma((CHIPS,)), dma((CHIPS,)),
            dma((4,)), dma((4,)),
        ],
        compiler_params=pltpu.CompilerParams(
            collective_id=0, has_side_effects=True, vmem_limit_bytes=67043328),
    )(lin_q, lin_k, lin_v, lin_gain.reshape(1, -1), soft_q, soft_k, soft_v)


def solution(mesh):
    split = P("seq", "grp")
    return jax.shard_map(
        shards,
        mesh=mesh,
        in_specs=(split, split, split, P("grp"), split, split, split),
        out_specs=(split, split),
        check_vma=False,
    )
```

```python
import functools

import jax
import jax.numpy as jnp
from jax import lax
from jax.experimental import pallas as pl
from jax.experimental.pallas import tpu as pltpu
from jax.sharding import PartitionSpec as P

HEADS = 64
HEAD_DIM = 128
EPSILON = 1e-06
MESH = pl.DeviceIdType.MESH
F32 = jnp.float32
BF16 = jnp.bfloat16

CHIPS = 16
SIDE = 4
ROWS = 256
SEQ = 8192
CHUNK = 1024
SCALE = HEAD_DIM ** -0.5
LOG2E = 1.4426950408889634


def kernel(
    lin_q, lin_k, lin_v, gain, soft_q, soft_k, soft_v,
    lin_out, soft_out,
    lq, lk, lv, mixed, state, half_in, chip_half, gathered, prefix_half, half_out, half_got,
    squares, kbuf, vbuf, qbuf, sbuf, pbuf, lbuf, mbuf,
    load_sem, k_send, k_recv, k_fwd, v_send, v_recv, v_fwd, q_send, q_recv, o_send, o_recv,
    x_sem, one_send, one_recv, two_send, two_recv, sq_send, sq_recv,
):
    me = lax.axis_index("seq")
    grp = lax.axis_index("grp")
    chip, core = me // 2, me % 2
    partner = chip * 2 + 1 - core
    y, z = chip // SIDE, chip % SIDE

    def chip_to(i):
        return (y + i // SIDE + i) % SIDE * SIDE + (z + i) % SIDE

    def chip_from(i):
        return (y + 2 * SIDE * SIDE - i // SIDE - i) % SIDE * SIDE + (z + SIDE * SIDE - i) % SIDE

    def cols(h):
        return pl.ds(pl.multiple_of(h * HEAD_DIM, HEAD_DIM), HEAD_DIM)

    def remote(src, dst, send, recv, seq):
        return pltpu.make_async_remote_copy(
            src_ref=src, dst_ref=dst, send_sem=send, recv_sem=recv,
            device_id={"seq": seq}, device_id_type=MESH)

    def arrived(dst, sem):
        pltpu.make_async_copy(dst, dst, sem).wait()

    loads = [pltpu.make_async_copy(src, dst, load_sem.at[n])
             for n, (src, dst) in enumerate(((lin_q, lq), (lin_k, lk), (lin_v, lv)))]
    for load in loads:
        load.start()

    barrier = pltpu.get_barrier_semaphore()

    @pl.loop(1, 2 * CHIPS)
    def _(i):
        pl.semaphore_signal(barrier, inc=1, device_id={"seq": lax.rem(me + i, 2 * CHIPS)}, device_id_type=MESH)

    for i in range(1, 4):
        pl.semaphore_signal(barrier, inc=1, device_id={"grp": lax.rem(grp + i, 4)}, device_id_type=MESH)

    pl.semaphore_wait(barrier, 2 * CHIPS - 1 + 3)

    def spread(src, buf, send, recv, fwd):
        pltpu.make_async_copy(src.at[:, cols(chip)], buf.at[me], recv.at[me]).start()
        remote(src.at[:, cols(chip)], buf.at[me], fwd.at[0], recv.at[me], partner).start()

        @pl.loop(1, CHIPS)
        def _(i):
            c = chip_to(i)
            remote(src.at[:, cols(c)], buf.at[me], send.at[i], recv.at[me], 2 * c + core).start()

    def forward(buf, recv, fwd):
        @pl.loop(1, CHIPS)
        def _(i):
            s = 2 * chip_from(i) + core
            arrived(buf.at[s], recv.at[s])
            remote(buf.at[s], buf.at[s], fwd.at[i], recv.at[s], partner).start()

        arrived(buf.at[me], recv.at[me])

        @pl.loop(0, CHIPS)
        def _(i):
            s = 2 * chip_from(i) + 1 - core
            arrived(buf.at[s], recv.at[s])

    def sent(buf, src, send, fwd):
        remote(src.at[:, cols(chip)], buf.at[me], fwd.at[0], fwd.at[0], partner).wait_send()

        @pl.loop(1, CHIPS)
        def _(i):
            remote(src.at[:, cols(0)], buf.at[me], send.at[i], send.at[i], partner).wait_send()
            remote(buf.at[me], buf.at[me], fwd.at[i], fwd.at[i], partner).wait_send()

    spread(soft_k, kbuf, k_send, k_recv, k_fwd)

    q_core = (core + chip) % 2

    @pl.when(q_core == core)
    def _():
        pltpu.make_async_copy(soft_q.at[:, cols(chip)], qbuf.at[chip], q_recv.at[chip]).start()

    @pl.when(q_core != core)
    def _():
        remote(soft_q.at[:, cols(chip)], qbuf.at[chip], q_send.at[0], q_recv.at[chip], partner).start()

    @pl.loop(1, CHIPS)
    def _(i):
        c = chip_to(i)
        remote(soft_q.at[:, cols(c)], qbuf.at[chip], q_send.at[i], q_recv.at[chip], 2 * c + q_core).start()

    for load in loads:
        load.wait()

    @pl.loop(0, CHIPS)
    def _(h):
        keys, values = lk[:, cols(h)], lv[:, cols(h)]
        state[h] = lax.dot_general(keys, values, (((0,), (0,)), ((), ())), preferred_element_type=F32)
        scores = lax.dot_general(lq[:, cols(h)], keys, (((1,), (1,)), ((), ())), preferred_element_type=F32)
        row = lax.broadcasted_iota(jnp.int32, (ROWS, ROWS), 0)
        col = lax.broadcasted_iota(jnp.int32, (ROWS, ROWS), 1)
        scores = jnp.where(col <= row, scores, 0.0)
        high = scores.astype(BF16)
        low = (scores - high.astype(F32)).astype(BF16)
        mixed[:, cols(h)] = (jnp.dot(high, values, preferred_element_type=F32)
                             + jnp.dot(low, values, preferred_element_type=F32))

    away = pl.ds(pl.multiple_of((1 - core) * 64, 64), 64)
    home = pl.ds(pl.multiple_of(core * 64, 64), 64)
    swap = remote(state.at[:, away, :], half_in, x_sem.at[0], x_sem.at[1], partner)
    swap.start()

    swap.wait()

    @pl.loop(0, CHIPS)
    def _(h):
        total = state[h, home, :] + half_in[h]
        chip_half[h] = total

        @pl.when(h == chip)
        def _():
            gathered[h] = total

    @pl.loop(1, CHIPS)
    def _(i):
        c = chip_to(i)
        remote(chip_half.at[c], gathered.at[chip], one_send.at[i], one_recv.at[chip], 2 * c + core).start()

    spread(soft_v, vbuf, v_send, v_recv, v_fwd)
    forward(kbuf, k_recv, k_fwd)

    def position(b):
        return 2 * b + (b + core) % 2

    def score(b, half, t, last, n, top):
        value = lax.dot_general(qbuf[b], kbuf[t * 4 + n], (((1,), (1,)), ((), ())), preferred_element_type=F32)
        if last:
            row = lax.broadcasted_iota(jnp.int32, (ROWS, ROWS), 0) + position(b) * ROWS
            col = lax.broadcasted_iota(jnp.int32, (ROWS, ROWS), 1) + (t * 4 + n) * ROWS
            value = jnp.where(col <= row, value, -1e30)
        sbuf[t + 1 - half, :, n * 256:(n + 1) * 256] = value
        most = jnp.maximum(value[:, :128], value[:, 128:])
        return most if top is None else jnp.maximum(top, most)

    def weigh(b, t, base, half, n):
        rows = slice(n * 64, (n + 1) * 64)
        top = mbuf[rows]
        total = lbuf[b, rows]
        for c in range(CHUNK // 128):
            part = slice(c * 128, (c + 1) * 128)
            expo = jnp.exp2(sbuf[t + 1 - half, rows, part] * (SCALE * LOG2E) - top)
            total = total + expo
            pbuf[base + t, half * ROWS + n * 64:half * ROWS + (n + 1) * 64, part] = expo.astype(BF16)
        lbuf[b, rows] = total

    def step(even, odd, t, base, last):
        top = None
        for n in range(4):
            if even is not None:
                weigh(even, t, base, 0, n)
            top = score(odd, 0 if even is None else 1, t, last, n, top)
        lbuf[odd] = jnp.maximum(lbuf[odd], top)

    def settle(b):
        top = jnp.max(lbuf[b], axis=1, keepdims=True) * (SCALE * LOG2E)
        mbuf[...] = jnp.broadcast_to(top, (ROWS, 128))
        lbuf[b] = jnp.zeros((ROWS, 128), F32)

    @pl.loop(0, CHIPS // 2)
    def _(i):
        pair = (chip // 2 + CHIPS // 2 - i) % (CHIPS // 2)
        even, odd = 2 * pair, 2 * pair + 1
        base = pair * (pair + 1) // 2
        for b in (even, odd):
            arrived(qbuf.at[b], q_recv.at[b])
            lbuf[b] = jnp.full((ROWS, 128), -1e30, F32)

        @pl.loop(0, pair)
        def _(t):
            step(None, even, t, base, False)

        step(None, even, pair, base, True)
        settle(even)

        @pl.loop(0, pair)
        def _(t):
            step(even, odd, t, base, False)

        step(even, odd, pair, base, True)
        settle(odd)

        @pl.loop(0, pair + 1)
        def _(t):
            for n in range(4):
                weigh(odd, t, base, 1, n)

        @pl.when(i == 4)
        def _():
            def running(c, total):
                @pl.when(c != chip)
                def _():
                    arrived(gathered.at[c], one_recv.at[c])

                own = gathered[c]
                gathered[c] = total

                @pl.when(c == chip)
                def _():
                    prefix_half[c] = total

                return total + own

            lax.fori_loop(0, CHIPS, running, jnp.zeros((64, HEAD_DIM), F32))

            @pl.loop(1, CHIPS)
            def _(i):
                c = chip_to(i)
                remote(gathered.at[c], prefix_half.at[chip], two_send.at[i], two_recv.at[chip], 2 * c + core).start()

        @pl.when(i == 6)
        def _():
            forward(vbuf, v_recv, v_fwd)

    @pl.loop(0, CHIPS // 2)
    def _(i):
        pair = (chip // 2 + CHIPS // 2 - i) % (CHIPS // 2)
        base = pair * (pair + 1) // 2
        sbuf[0:2, :, 0:128] = jnp.zeros((2, ROWS, HEAD_DIM), F32)

        @pl.loop(0, pair + 1)
        def _(t):
            values = vbuf[pl.ds(t * 4, 4)].reshape(CHUNK, HEAD_DIM)
            out = jnp.dot(pbuf[base + t], values, preferred_element_type=F32)
            sbuf[0:2, :, 0:128] += out.reshape(2, ROWS, HEAD_DIM)

        for half in range(2):
            b = 2 * pair + half
            s = position(b)
            qbuf[b] = (sbuf[half, :, 0:128] / jnp.sum(lbuf[b], axis=1, keepdims=True)).astype(BF16)

            @pl.when(s == me)
            def _():
                pltpu.make_async_copy(qbuf.at[b], soft_out.at[:, cols(chip)], o_recv.at[chip]).start()

            @pl.when(s != me)
            def _():
                remote(qbuf.at[b], soft_out.at[:, cols(chip)], o_send.at[b], o_recv.at[chip], s).start()

    @pl.loop(0, CHIPS)
    def _(h):
        @pl.when(h != chip)
        def _():
            arrived(prefix_half.at[h], two_recv.at[h])

    first = jnp.where(core == 0, 1.0, 0.0).astype(F32)
    half_out[...] = prefix_half[...] + first * state[:, 0:64, :]
    swap_two = remote(half_out, half_got, x_sem.at[2], x_sem.at[3], partner)
    swap_two.start()
    state[:, home, :] = prefix_half[...] + (1.0 - first) * half_in[...]
    swap_two.wait()
    state[:, away, :] = half_got[...]
    squares[0] = jnp.zeros((ROWS, 128), F32)

    @pl.loop(0, CHIPS)
    def _(h):
        full = state[h]
        high = full.astype(BF16)
        low = (full - high.astype(F32)).astype(BF16)
        queries = lq[:, cols(h)]
        out = (mixed[:, cols(h)] + jnp.dot(queries, high, preferred_element_type=F32)
               + jnp.dot(queries, low, preferred_element_type=F32))
        mixed[:, cols(h)] = out
        squares[0] += out * out

    swaps = []
    for i in range(1, 4):
        copy = pltpu.make_async_remote_copy(
            src_ref=squares.at[0], dst_ref=squares.at[i], send_sem=sq_send.at[i], recv_sem=sq_recv.at[i],
            device_id={"grp": lax.rem(grp + i, 4)}, device_id_type=MESH)
        copy.start()
        swaps.append(copy)
    for copy in swaps:
        copy.wait()
    total = squares[0] + squares[1] + squares[2] + squares[3]
    inverse = lax.rsqrt(jnp.sum(total, axis=1, keepdims=True) / (HEADS * HEAD_DIM) + EPSILON)
    mbuf[...] = jnp.broadcast_to(inverse, (ROWS, 128))

    @pl.loop(0, CHIPS)
    def _(h):
        lk[:, cols(h)] = (mixed[:, cols(h)] * mbuf[...] * gain[:, cols(h)]).astype(BF16)

    store = pltpu.make_async_copy(lk, lin_out, load_sem.at[3])
    store.start()

    sent(kbuf, soft_k, k_send, k_fwd)
    sent(vbuf, soft_v, v_send, v_fwd)

    @pl.when(q_core != core)
    def _():
        remote(soft_q.at[:, cols(0)], qbuf.at[0], q_send.at[0], q_send.at[0], partner).wait_send()

    @pl.loop(1, CHIPS)
    def _(i):
        remote(soft_q.at[:, cols(0)], qbuf.at[0], q_send.at[i], q_send.at[i], partner).wait_send()
        remote(chip_half.at[0], chip_half.at[0], one_send.at[i], one_send.at[i], partner).wait_send()
        remote(chip_half.at[0], chip_half.at[0], two_send.at[i], two_send.at[i], partner).wait_send()

    @pl.loop(0, CHIPS)
    def _(b):
        @pl.when(position(b) != me)
        def _():
            remote(qbuf.at[0], qbuf.at[0], o_send.at[b], o_send.at[b], partner).wait_send()

        arrived(soft_out.at[:, cols(b)], o_recv.at[b])

    store.wait()


def shards(lin_q, lin_k, lin_v, lin_gain, soft_q, soft_k, soft_v):
    half = pltpu.VMEM((CHIPS, 64, HEAD_DIM), F32)
    tokens = pltpu.VMEM((ROWS, CHIPS * HEAD_DIM), BF16)
    dma = pltpu.SemaphoreType.DMA
    hbm = pl.BlockSpec(memory_space=pl.ANY)
    shape = jax.ShapeDtypeStruct(lin_q.shape, BF16)
    return pl.pallas_call(
        kernel,
        out_shape=(shape, shape),
        in_specs=[hbm, hbm, hbm, pl.BlockSpec(memory_space=pltpu.VMEM), hbm, hbm, hbm],
        out_specs=(hbm, hbm),
        scratch_shapes=[
            tokens, tokens, tokens,
            pltpu.VMEM((ROWS, CHIPS * HEAD_DIM), F32),
            pltpu.VMEM((CHIPS, HEAD_DIM, HEAD_DIM), F32),
            half, half, half, half, half, half,
            pltpu.VMEM((4, ROWS, 128), F32),
            pltpu.VMEM((2 * CHIPS, ROWS, HEAD_DIM), BF16),
            pltpu.VMEM((2 * CHIPS, ROWS, HEAD_DIM), BF16),
            pltpu.VMEM((CHIPS, ROWS, HEAD_DIM), BF16),
            pltpu.VMEM((SEQ // CHUNK + 1, ROWS, CHUNK), F32),
            pltpu.VMEM((36, 2 * ROWS, CHUNK), BF16),
            pltpu.VMEM((CHIPS, ROWS, 128), F32),
            pltpu.VMEM((ROWS, 128), F32),
            dma((4,)),
            dma((CHIPS,)), dma((2 * CHIPS,)), dma((CHIPS,)),
            dma((CHIPS,)), dma((2 * CHIPS,)), dma((CHIPS,)),
            dma((CHIPS,)), dma((CHIPS,)),
            dma((CHIPS,)), dma((CHIPS,)),
            dma((4,)),
            dma((CHIPS,)), dma((CHIPS,)),
            dma((CHIPS,)), dma((CHIPS,)),
            dma((4,)), dma((4,)),
        ],
        compiler_params=pltpu.CompilerParams(
            collective_id=0, has_side_effects=True, vmem_limit_bytes=67043328),
    )(lin_q, lin_k, lin_v, lin_gain.reshape(1, -1), soft_q, soft_k, soft_v)


def solution(mesh):
    split = P("seq", "grp")
    return jax.shard_map(
        shards,
        mesh=mesh,
        in_specs=(split, split, split, P("grp"), split, split, split),
        out_specs=(split, split),
        check_vma=False,
    )
```

```python
import functools

import jax
import jax.numpy as jnp
from jax import lax
from jax.experimental import pallas as pl
from jax.experimental.pallas import tpu as pltpu
from jax.sharding import PartitionSpec as P

HEADS = 64
HEAD_DIM = 128
EPSILON = 1e-06
MESH = pl.DeviceIdType.MESH
F32 = jnp.float32
BF16 = jnp.bfloat16

CHIPS = 16
SIDE = 4
ROWS = 256
SEQ = 8192
CHUNK = 1024
SCALE = HEAD_DIM ** -0.5
LOG2E = 1.4426950408889634


def kernel(
    lin_q, lin_k, lin_v, gain, soft_q, soft_k, soft_v,
    lin_out, soft_out,
    lq, lk, lv, mixed, state, half_in, chip_half, gathered, prefix_half, half_out, half_got,
    squares, kbuf, vbuf, qbuf, sbuf, pbuf, lbuf, mbuf,
    load_sem, k_send, k_recv, k_fwd, v_send, v_recv, v_fwd, q_send, q_recv, o_send, o_recv,
    x_sem, one_send, one_recv, two_send, two_recv, sq_send, sq_recv,
):
    me = lax.axis_index("seq")
    grp = lax.axis_index("grp")
    chip, core = me // 2, me % 2
    partner = chip * 2 + 1 - core
    y, z = chip // SIDE, chip % SIDE

    def chip_to(i):
        return (y + i // SIDE + i) % SIDE * SIDE + (z + i) % SIDE

    def chip_from(i):
        return (y + 2 * SIDE * SIDE - i // SIDE - i) % SIDE * SIDE + (z + SIDE * SIDE - i) % SIDE

    def pair_from(i):
        return (y + 12 - i // 2 * 3 - i % 2 * 2) % SIDE * 2 + (z // 2 + i) % 2

    def query_to(j):
        i = j // 2
        return (y + i // 2 * 3 + i % 2 * 2) % SIDE * SIDE + (z // 2 + i) % 2 * 2 + j % 2

    def cols(h):
        return pl.ds(pl.multiple_of(h * HEAD_DIM, HEAD_DIM), HEAD_DIM)

    def remote(src, dst, send, recv, seq):
        return pltpu.make_async_remote_copy(
            src_ref=src, dst_ref=dst, send_sem=send, recv_sem=recv,
            device_id={"seq": seq}, device_id_type=MESH)

    def arrived(dst, sem):
        pltpu.make_async_copy(dst, dst, sem).wait()

    loads = [pltpu.make_async_copy(src, dst, load_sem.at[n])
             for n, (src, dst) in enumerate(((lin_q, lq), (lin_k, lk), (lin_v, lv)))]
    for load in loads:
        load.start()

    barrier = pltpu.get_barrier_semaphore()

    @pl.loop(1, 2 * CHIPS)
    def _(i):
        pl.semaphore_signal(barrier, inc=1, device_id={"seq": lax.rem(me + i, 2 * CHIPS)}, device_id_type=MESH)

    for i in range(1, 4):
        pl.semaphore_signal(barrier, inc=1, device_id={"grp": lax.rem(grp + i, 4)}, device_id_type=MESH)

    pl.semaphore_wait(barrier, 2 * CHIPS - 1 + 3)

    def spread(src, buf, send, recv, fwd):
        pltpu.make_async_copy(src.at[:, cols(chip)], buf.at[me], recv.at[me]).start()
        remote(src.at[:, cols(chip)], buf.at[me], fwd.at[0], recv.at[me], partner).start()

        @pl.loop(1, CHIPS)
        def _(i):
            c = chip_to(i)
            remote(src.at[:, cols(c)], buf.at[me], send.at[i], recv.at[me], 2 * c + core).start()

    def forward(buf, recv, fwd):
        @pl.loop(1, CHIPS)
        def _(i):
            s = 2 * chip_from(i) + core
            arrived(buf.at[s], recv.at[s])
            remote(buf.at[s], buf.at[s], fwd.at[i], recv.at[s], partner).start()

        arrived(buf.at[me], recv.at[me])

        @pl.loop(0, CHIPS)
        def _(i):
            s = 2 * chip_from(i) + 1 - core
            arrived(buf.at[s], recv.at[s])

    def sent(buf, src, send, fwd):
        remote(src.at[:, cols(chip)], buf.at[me], fwd.at[0], fwd.at[0], partner).wait_send()

        @pl.loop(1, CHIPS)
        def _(i):
            remote(src.at[:, cols(0)], buf.at[me], send.at[i], send.at[i], partner).wait_send()
            remote(buf.at[me], buf.at[me], fwd.at[i], fwd.at[i], partner).wait_send()

    spread(soft_k, kbuf, k_send, k_recv, k_fwd)

    q_core = (core + chip) % 2

    @pl.when(q_core == core)
    def _():
        pltpu.make_async_copy(soft_q.at[:, cols(chip)], qbuf.at[chip], q_recv.at[chip]).start()

    @pl.when(q_core != core)
    def _():
        remote(soft_q.at[:, cols(chip)], qbuf.at[chip], q_send.at[0], q_recv.at[chip], partner).start()

    beside = chip + 1 - chip % 2 * 2
    remote(soft_q.at[:, cols(beside)], qbuf.at[chip], q_send.at[1], q_recv.at[chip], 2 * beside + q_core).start()

    @pl.loop(2, CHIPS)
    def _(j):
        c = query_to(j)
        remote(soft_q.at[:, cols(c)], qbuf.at[chip], q_send.at[j], q_recv.at[chip], 2 * c + q_core).start()

    for load in loads:
        load.wait()

    @pl.loop(0, CHIPS)
    def _(h):
        keys, values = lk[:, cols(h)], lv[:, cols(h)]
        state[h] = lax.dot_general(keys, values, (((0,), (0,)), ((), ())), preferred_element_type=F32)
        scores = lax.dot_general(lq[:, cols(h)], keys, (((1,), (1,)), ((), ())), preferred_element_type=F32)
        row = lax.broadcasted_iota(jnp.int32, (ROWS, ROWS), 0)
        col = lax.broadcasted_iota(jnp.int32, (ROWS, ROWS), 1)
        scores = jnp.where(col <= row, scores, 0.0)
        high = scores.astype(BF16)
        low = (scores - high.astype(F32)).astype(BF16)
        mixed[:, cols(h)] = (jnp.dot(high, values, preferred_element_type=F32)
                             + jnp.dot(low, values, preferred_element_type=F32))

    away = pl.ds(pl.multiple_of((1 - core) * 64, 64), 64)
    home = pl.ds(pl.multiple_of(core * 64, 64), 64)
    swap = remote(state.at[:, away, :], half_in, x_sem.at[0], x_sem.at[1], partner)
    swap.start()

    swap.wait()

    @pl.loop(0, CHIPS)
    def _(h):
        total = state[h, home, :] + half_in[h]
        chip_half[h] = total

        @pl.when(h == chip)
        def _():
            gathered[h] = total

    @pl.loop(1, CHIPS)
    def _(i):
        c = chip_to(i)
        remote(chip_half.at[c], gathered.at[chip], one_send.at[i], one_recv.at[chip], 2 * c + core).start()

    spread(soft_v, vbuf, v_send, v_recv, v_fwd)
    forward(kbuf, k_recv, k_fwd)

    def position(b):
        return 2 * b + (b + core) % 2

    def score(b, half, t, last, n, top):
        value = lax.dot_general(qbuf[b], kbuf[t * 4 + n], (((1,), (1,)), ((), ())), preferred_element_type=F32)
        if last:
            row = lax.broadcasted_iota(jnp.int32, (ROWS, ROWS), 0) + position(b) * ROWS
            col = lax.broadcasted_iota(jnp.int32, (ROWS, ROWS), 1) + (t * 4 + n) * ROWS
            value = jnp.where(col <= row, value, -1e30)
        sbuf[t + 1 - half, :, n * 256:(n + 1) * 256] = value
        most = jnp.maximum(value[:, :128], value[:, 128:])
        return most if top is None else jnp.maximum(top, most)

    def weigh(b, t, base, half, n):
        rows = slice(n * 32, (n + 1) * 32)
        top = mbuf[rows]
        total = lbuf[b, rows]
        for c in range(CHUNK // 128):
            part = slice(c * 128, (c + 1) * 128)
            expo = jnp.exp2(sbuf[t + 1 - half, rows, part] * (SCALE * LOG2E) - top)
            total = total + expo
            pbuf[base + t, half * ROWS + n * 32:half * ROWS + (n + 1) * 32, part] = expo.astype(BF16)
        lbuf[b, rows] = total

    def step(even, odd, t, base, last):
        top = None
        if even is not None:
            for n in range(8):
                weigh(even, t, base, 0, n)
        for n in range(4):
            top = score(odd, 0 if even is None else 1, t, last, n, top)
        lbuf[odd] = jnp.maximum(lbuf[odd], top)

    def settle(b):
        top = jnp.max(lbuf[b], axis=1, keepdims=True) * (SCALE * LOG2E)
        mbuf[...] = jnp.broadcast_to(top, (ROWS, 128))
        lbuf[b] = jnp.zeros((ROWS, 128), F32)

    @pl.loop(0, CHIPS // 2)
    def _(i):
        pair = pair_from(i)
        even, odd = 2 * pair, 2 * pair + 1
        base = pair * (pair + 1) // 2
        for b in (even, odd):
            arrived(qbuf.at[b], q_recv.at[b])
            lbuf[b] = jnp.full((ROWS, 128), -1e30, F32)

        @pl.loop(0, pair)
        def _(t):
            step(None, even, t, base, False)

        step(None, even, pair, base, True)
        settle(even)

        @pl.loop(0, pair)
        def _(t):
            step(even, odd, t, base, False)

        step(even, odd, pair, base, True)
        settle(odd)

        @pl.loop(0, pair + 1)
        def _(t):
            for n in range(8):
                weigh(odd, t, base, 1, n)

        @pl.when(i == 4)
        def _():
            def running(c, total):
                @pl.when(c != chip)
                def _():
                    arrived(gathered.at[c], one_recv.at[c])

                own = gathered[c]
                gathered[c] = total

                @pl.when(c == chip)
                def _():
                    prefix_half[c] = total

                return total + own

            lax.fori_loop(0, CHIPS, running, jnp.zeros((64, HEAD_DIM), F32))

            @pl.loop(1, CHIPS)
            def _(i):
                c = chip_to(i)
                remote(gathered.at[c], prefix_half.at[chip], two_send.at[i], two_recv.at[chip], 2 * c + core).start()

        @pl.when(i == 6)
        def _():
            forward(vbuf, v_recv, v_fwd)

    @pl.loop(0, CHIPS)
    def _(h):
        @pl.when(h != chip)
        def _():
            arrived(prefix_half.at[h], two_recv.at[h])

    first = jnp.where(core == 0, 1.0, 0.0).astype(F32)
    half_out[...] = prefix_half[...] + first * state[:, 0:64, :]
    state[:, home, :] = prefix_half[...] + (1.0 - first) * half_in[...]
    swap_two = remote(half_out, half_got, x_sem.at[2], x_sem.at[3], partner)
    swap_two.start()

    def squares_to(i):
        return pltpu.make_async_remote_copy(
            src_ref=squares.at[0], dst_ref=squares.at[i], send_sem=sq_send.at[i], recv_sem=sq_recv.at[i],
            device_id={"grp": lax.rem(grp + i, 4)}, device_id_type=MESH)

    store = pltpu.make_async_copy(lk, lin_out, load_sem.at[3])

    def carry():
        swap_two.wait()
        state[:, away, :] = half_got[...]
        squares[0] = jnp.zeros((ROWS, 128), F32)

        @pl.loop(0, CHIPS)
        def _(h):
            full = state[h]
            high = full.astype(BF16)
            low = (full - high.astype(F32)).astype(BF16)
            queries = lq[:, cols(h)]
            out = (mixed[:, cols(h)] + jnp.dot(queries, high, preferred_element_type=F32)
                   + jnp.dot(queries, low, preferred_element_type=F32))
            mixed[:, cols(h)] = out
            squares[0] += out * out

        for i in range(1, 4):
            squares_to(i).start()

    def normalize():
        for i in range(1, 4):
            squares_to(i).wait()
        total = squares[0] + squares[1] + squares[2] + squares[3]
        inverse = lax.rsqrt(jnp.sum(total, axis=1, keepdims=True) / (HEADS * HEAD_DIM) + EPSILON)
        mbuf[...] = jnp.broadcast_to(inverse, (ROWS, 128))

        @pl.loop(0, CHIPS)
        def _(h):
            lk[:, cols(h)] = (mixed[:, cols(h)] * mbuf[...] * gain[:, cols(h)]).astype(BF16)

        store.start()

    @pl.loop(0, CHIPS // 2)
    def _(i):
        pair = pair_from(i)
        base = pair * (pair + 1) // 2
        sbuf[0:2, :, 0:128] = jnp.zeros((2, ROWS, HEAD_DIM), F32)

        @pl.loop(0, pair + 1)
        def _(t):
            values = vbuf[pl.ds(t * 4, 4)].reshape(CHUNK, HEAD_DIM)
            out = jnp.dot(pbuf[base + t], values, preferred_element_type=F32)
            sbuf[0:2, :, 0:128] += out.reshape(2, ROWS, HEAD_DIM)

        for half in range(2):
            b = 2 * pair + half
            s = position(b)
            qbuf[b] = (sbuf[half, :, 0:128] / jnp.sum(lbuf[b], axis=1, keepdims=True)).astype(BF16)

            @pl.when(s == me)
            def _():
                pltpu.make_async_copy(qbuf.at[b], soft_out.at[:, cols(chip)], o_recv.at[chip]).start()

            @pl.when(s != me)
            def _():
                remote(qbuf.at[b], soft_out.at[:, cols(chip)], o_send.at[b], o_recv.at[chip], s).start()

        pl.when(i == 1)(carry)
        pl.when(i == 4)(normalize)

    sent(kbuf, soft_k, k_send, k_fwd)
    sent(vbuf, soft_v, v_send, v_fwd)

    @pl.when(q_core != core)
    def _():
        remote(soft_q.at[:, cols(0)], qbuf.at[0], q_send.at[0], q_send.at[0], partner).wait_send()

    @pl.loop(1, CHIPS)
    def _(i):
        remote(soft_q.at[:, cols(0)], qbuf.at[0], q_send.at[i], q_send.at[i], partner).wait_send()
        remote(chip_half.at[0], chip_half.at[0], one_send.at[i], one_send.at[i], partner).wait_send()
        remote(chip_half.at[0], chip_half.at[0], two_send.at[i], two_send.at[i], partner).wait_send()

    @pl.loop(0, CHIPS)
    def _(b):
        @pl.when(position(b) != me)
        def _():
            remote(qbuf.at[0], qbuf.at[0], o_send.at[b], o_send.at[b], partner).wait_send()

        arrived(soft_out.at[:, cols(b)], o_recv.at[b])

    store.wait()


def shards(lin_q, lin_k, lin_v, lin_gain, soft_q, soft_k, soft_v):
    half = pltpu.VMEM((CHIPS, 64, HEAD_DIM), F32)
    tokens = pltpu.VMEM((ROWS, CHIPS * HEAD_DIM), BF16)
    dma = pltpu.SemaphoreType.DMA
    hbm = pl.BlockSpec(memory_space=pl.ANY)
    shape = jax.ShapeDtypeStruct(lin_q.shape, BF16)
    return pl.pallas_call(
        kernel,
        out_shape=(shape, shape),
        in_specs=[hbm, hbm, hbm, pl.BlockSpec(memory_space=pltpu.VMEM), hbm, hbm, hbm],
        out_specs=(hbm, hbm),
        scratch_shapes=[
            tokens, tokens, tokens,
            pltpu.VMEM((ROWS, CHIPS * HEAD_DIM), F32),
            pltpu.VMEM((CHIPS, HEAD_DIM, HEAD_DIM), F32),
            half, half, half, half, half, half,
            pltpu.VMEM((4, ROWS, 128), F32),
            pltpu.VMEM((2 * CHIPS, ROWS, HEAD_DIM), BF16),
            pltpu.VMEM((2 * CHIPS, ROWS, HEAD_DIM), BF16),
            pltpu.VMEM((CHIPS, ROWS, HEAD_DIM), BF16),
            pltpu.VMEM((SEQ // CHUNK + 1, ROWS, CHUNK), F32),
            pltpu.VMEM((36, 2 * ROWS, CHUNK), BF16),
            pltpu.VMEM((CHIPS, ROWS, 128), F32),
            pltpu.VMEM((ROWS, 128), F32),
            dma((4,)),
            dma((CHIPS,)), dma((2 * CHIPS,)), dma((CHIPS,)),
            dma((CHIPS,)), dma((2 * CHIPS,)), dma((CHIPS,)),
            dma((CHIPS,)), dma((CHIPS,)),
            dma((CHIPS,)), dma((CHIPS,)),
            dma((4,)),
            dma((CHIPS,)), dma((CHIPS,)),
            dma((CHIPS,)), dma((CHIPS,)),
            dma((4,)), dma((4,)),
        ],
        compiler_params=pltpu.CompilerParams(
            collective_id=0, has_side_effects=True, vmem_limit_bytes=67043328),
    )(lin_q, lin_k, lin_v, lin_gain.reshape(1, -1), soft_q, soft_k, soft_v)


def solution(mesh):
    split = P("seq", "grp")
    return jax.shard_map(
        shards,
        mesh=mesh,
        in_specs=(split, split, split, P("grp"), split, split, split),
        out_specs=(split, split),
        check_vma=False,
    )
```

```python
import functools

import jax
import jax.numpy as jnp
from jax import lax
from jax.experimental import pallas as pl
from jax.experimental.pallas import tpu as pltpu
from jax.sharding import PartitionSpec as P

HEADS = 64
HEAD_DIM = 128
EPSILON = 1e-06
MESH = pl.DeviceIdType.MESH
F32 = jnp.float32
BF16 = jnp.bfloat16

CHIPS = 16
SIDE = 4
ROWS = 256
SEQ = 8192
CHUNK = 1024
SCALE = HEAD_DIM ** -0.5
LOG2E = 1.4426950408889634


def kernel(
    lin_q, lin_k, lin_v, gain, soft_q, soft_k, soft_v,
    lin_out, soft_out,
    lq, lk, lv, mixed, state, half_in, chip_half, gathered, prefix_half, half_out, half_got,
    squares, kbuf, vbuf, qbuf, sbuf, pbuf, lbuf, mbuf,
    load_sem, k_send, k_recv, k_fwd, v_send, v_recv, v_fwd, q_send, q_recv, o_send, o_recv,
    x_sem, one_send, one_recv, two_send, two_recv, sq_send, sq_recv,
):
    me = lax.axis_index("seq")
    grp = lax.axis_index("grp")
    chip, core = me // 2, me % 2
    partner = chip * 2 + 1 - core
    y, z = chip // SIDE, chip % SIDE

    def chip_to(i):
        return (y + i // SIDE + i) % SIDE * SIDE + (z + i) % SIDE

    def chip_from(i):
        return (y + 2 * SIDE * SIDE - i // SIDE - i) % SIDE * SIDE + (z + SIDE * SIDE - i) % SIDE

    def pair_from(i):
        return (y + 12 - i // 2 * 3 - i % 2 * 2) % SIDE * 2 + (z // 2 + i) % 2

    def query_to(j):
        i = j // 2
        return (y + i // 2 * 3 + i % 2 * 2) % SIDE * SIDE + (z // 2 + i) % 2 * 2 + j % 2

    def cols(h):
        return pl.ds(pl.multiple_of(h * HEAD_DIM, HEAD_DIM), HEAD_DIM)

    def remote(src, dst, send, recv, seq):
        return pltpu.make_async_remote_copy(
            src_ref=src, dst_ref=dst, send_sem=send, recv_sem=recv,
            device_id={"seq": seq}, device_id_type=MESH)

    def arrived(dst, sem):
        pltpu.make_async_copy(dst, dst, sem).wait()

    loads = [pltpu.make_async_copy(src, dst, load_sem.at[n])
             for n, (src, dst) in enumerate(((lin_q, lq), (lin_k, lk), (lin_v, lv)))]
    for load in loads:
        load.start()

    barrier = pltpu.get_barrier_semaphore()

    @pl.loop(1, 2 * CHIPS)
    def _(i):
        pl.semaphore_signal(barrier, inc=1, device_id={"seq": lax.rem(me + i, 2 * CHIPS)}, device_id_type=MESH)

    for i in range(1, 4):
        pl.semaphore_signal(barrier, inc=1, device_id={"grp": lax.rem(grp + i, 4)}, device_id_type=MESH)

    pl.semaphore_wait(barrier, 2 * CHIPS - 1 + 3)

    def spread(src, buf, send, recv, fwd):
        pltpu.make_async_copy(src.at[:, cols(chip)], buf.at[me], recv.at[me]).start()
        remote(src.at[:, cols(chip)], buf.at[me], fwd.at[0], recv.at[me], partner).start()

        @pl.loop(1, CHIPS)
        def _(i):
            c = chip_to(i)
            remote(src.at[:, cols(c)], buf.at[me], send.at[i], recv.at[me], 2 * c + core).start()

    def forward(buf, recv, fwd):
        @pl.loop(1, CHIPS)
        def _(i):
            s = 2 * chip_from(i) + core
            arrived(buf.at[s], recv.at[s])
            remote(buf.at[s], buf.at[s], fwd.at[i], recv.at[s], partner).start()

        arrived(buf.at[me], recv.at[me])

        @pl.loop(0, CHIPS)
        def _(i):
            s = 2 * chip_from(i) + 1 - core
            arrived(buf.at[s], recv.at[s])

    def sent(buf, src, send, fwd):
        remote(src.at[:, cols(chip)], buf.at[me], fwd.at[0], fwd.at[0], partner).wait_send()

        @pl.loop(1, CHIPS)
        def _(i):
            remote(src.at[:, cols(0)], buf.at[me], send.at[i], send.at[i], partner).wait_send()
            remote(buf.at[me], buf.at[me], fwd.at[i], fwd.at[i], partner).wait_send()

    spread(soft_k, kbuf, k_send, k_recv, k_fwd)

    q_core = (core + chip) % 2

    @pl.when(q_core == core)
    def _():
        pltpu.make_async_copy(soft_q.at[:, cols(chip)], qbuf.at[chip], q_recv.at[chip]).start()

    @pl.when(q_core != core)
    def _():
        remote(soft_q.at[:, cols(chip)], qbuf.at[chip], q_send.at[0], q_recv.at[chip], partner).start()

    beside = chip + 1 - chip % 2 * 2
    remote(soft_q.at[:, cols(beside)], qbuf.at[chip], q_send.at[1], q_recv.at[chip], 2 * beside + q_core).start()

    @pl.loop(2, CHIPS)
    def _(j):
        c = query_to(j)
        remote(soft_q.at[:, cols(c)], qbuf.at[chip], q_send.at[j], q_recv.at[chip], 2 * c + q_core).start()

    for load in loads:
        load.wait()

    @pl.loop(0, CHIPS)
    def _(h):
        keys, values = lk[:, cols(h)], lv[:, cols(h)]
        state[h] = lax.dot_general(keys, values, (((0,), (0,)), ((), ())), preferred_element_type=F32)
        scores = lax.dot_general(lq[:, cols(h)], keys, (((1,), (1,)), ((), ())), preferred_element_type=F32)
        row = lax.broadcasted_iota(jnp.int32, (ROWS, ROWS), 0)
        col = lax.broadcasted_iota(jnp.int32, (ROWS, ROWS), 1)
        scores = jnp.where(col <= row, scores, 0.0)
        high = scores.astype(BF16)
        low = (scores - high.astype(F32)).astype(BF16)
        mixed[:, cols(h)] = (jnp.dot(high, values, preferred_element_type=F32)
                             + jnp.dot(low, values, preferred_element_type=F32))

    away = pl.ds(pl.multiple_of((1 - core) * 64, 64), 64)
    home = pl.ds(pl.multiple_of(core * 64, 64), 64)
    swap = remote(state.at[:, away, :], half_in, x_sem.at[0], x_sem.at[1], partner)
    swap.start()

    swap.wait()

    @pl.loop(0, CHIPS)
    def _(h):
        total = state[h, home, :] + half_in[h]
        chip_half[h] = total

        @pl.when(h == chip)
        def _():
            gathered[h] = total

    @pl.loop(1, CHIPS)
    def _(i):
        c = chip_to(i)
        remote(chip_half.at[c], gathered.at[chip], one_send.at[i], one_recv.at[chip], 2 * c + core).start()

    spread(soft_v, vbuf, v_send, v_recv, v_fwd)
    forward(kbuf, k_recv, k_fwd)

    def position(b):
        return 2 * b + (b + core) % 2

    def score(b, half, t, last, n, top):
        value = lax.dot_general(qbuf[b], kbuf[t * 4 + n], (((1,), (1,)), ((), ())), preferred_element_type=F32)
        if last:
            row = lax.broadcasted_iota(jnp.int32, (ROWS, ROWS), 0) + position(b) * ROWS
            col = lax.broadcasted_iota(jnp.int32, (ROWS, ROWS), 1) + (t * 4 + n) * ROWS
            value = jnp.where(col <= row, value, -1e30)
        sbuf[t + 1 - half, :, n * 256:(n + 1) * 256] = value
        most = jnp.maximum(value[:, :128], value[:, 128:])
        return most if top is None else jnp.maximum(top, most)

    def weigh(b, t, base, half, n):
        rows = slice(n * 32, (n + 1) * 32)
        top = mbuf[rows]
        total = lbuf[b, rows]
        for c in range(CHUNK // 128):
            part = slice(c * 128, (c + 1) * 128)
            expo = jnp.exp2(sbuf[t + 1 - half, rows, part] * (SCALE * LOG2E) - top)
            total = total + expo
            pbuf[base + t, half * ROWS + n * 32:half * ROWS + (n + 1) * 32, part] = expo.astype(BF16)
        lbuf[b, rows] = total

    def weigh_all(b, t, base, half):
        for n in range(8):
            weigh(b, t, base, half, n)

    def step(b, half, t, last):
        top = None
        for n in range(4):
            top = score(b, half, t, last, n, top)
        lbuf[b] = jnp.maximum(lbuf[b], top)

    def settle(b):
        top = jnp.max(lbuf[b], axis=1, keepdims=True) * (SCALE * LOG2E)
        mbuf[...] = jnp.broadcast_to(top, (ROWS, 128))
        lbuf[b] = jnp.zeros((ROWS, 128), F32)

    @pl.loop(0, CHIPS // 2)
    def _(i):
        pair = pair_from(i)
        even, odd = 2 * pair, 2 * pair + 1
        base = pair * (pair + 1) // 2
        before = pair_from(jnp.maximum(i - 1, 0))
        old, old_base = 2 * before + 1, before * (before + 1) // 2
        left = jnp.where(i == 0, 0, before + 1)
        both = jnp.minimum(pair, left)
        for b in (even, odd):
            arrived(qbuf.at[b], q_recv.at[b])
            lbuf[b] = jnp.full((ROWS, 128), -1e30, F32)

        @pl.loop(0, left - both)
        def _(t):
            weigh_all(old, both + t, old_base, 1)

        step(even, 0, pair, True)

        @pl.loop(0, pair - both)
        def _(t):
            step(even, 0, both + t, False)

        @pl.loop(0, both)
        def _(t):
            weigh_all(old, both - 1 - t, old_base, 1)
            step(even, 0, both - 1 - t, False)

        settle(even)

        @pl.loop(0, pair)
        def _(t):
            weigh_all(even, t, base, 0)
            step(odd, 1, t, False)

        weigh_all(even, pair, base, 0)
        step(odd, 1, pair, True)
        settle(odd)

        @pl.when(i == 4)
        def _():
            def running(c, total):
                @pl.when(c != chip)
                def _():
                    arrived(gathered.at[c], one_recv.at[c])

                own = gathered[c]
                gathered[c] = total

                @pl.when(c == chip)
                def _():
                    prefix_half[c] = total

                return total + own

            lax.fori_loop(0, CHIPS, running, jnp.zeros((64, HEAD_DIM), F32))

            @pl.loop(1, CHIPS)
            def _(i):
                c = chip_to(i)
                remote(gathered.at[c], prefix_half.at[chip], two_send.at[i], two_recv.at[chip], 2 * c + core).start()

        @pl.when(i == 6)
        def _():
            forward(vbuf, v_recv, v_fwd)

    final = pair_from(CHIPS // 2 - 1)

    @pl.loop(0, final + 1)
    def _(t):
        weigh_all(2 * final + 1, t, final * (final + 1) // 2, 1)

    @pl.loop(0, CHIPS)
    def _(h):
        @pl.when(h != chip)
        def _():
            arrived(prefix_half.at[h], two_recv.at[h])

    first = jnp.where(core == 0, 1.0, 0.0).astype(F32)
    half_out[...] = prefix_half[...] + first * state[:, 0:64, :]
    state[:, home, :] = prefix_half[...] + (1.0 - first) * half_in[...]
    swap_two = remote(half_out, half_got, x_sem.at[2], x_sem.at[3], partner)
    swap_two.start()

    def squares_to(i):
        return pltpu.make_async_remote_copy(
            src_ref=squares.at[0], dst_ref=squares.at[i], send_sem=sq_send.at[i], recv_sem=sq_recv.at[i],
            device_id={"grp": lax.rem(grp + i, 4)}, device_id_type=MESH)

    store = pltpu.make_async_copy(lk, lin_out, load_sem.at[3])

    def carry():
        swap_two.wait()
        state[:, away, :] = half_got[...]
        squares[0] = jnp.zeros((ROWS, 128), F32)

        @pl.loop(0, CHIPS)
        def _(h):
            full = state[h]
            high = full.astype(BF16)
            low = (full - high.astype(F32)).astype(BF16)
            queries = lq[:, cols(h)]
            out = (mixed[:, cols(h)] + jnp.dot(queries, high, preferred_element_type=F32)
                   + jnp.dot(queries, low, preferred_element_type=F32))
            mixed[:, cols(h)] = out
            squares[0] += out * out

        for i in range(1, 4):
            squares_to(i).start()

    def normalize():
        for i in range(1, 4):
            squares_to(i).wait()
        total = squares[0] + squares[1] + squares[2] + squares[3]
        inverse = lax.rsqrt(jnp.sum(total, axis=1, keepdims=True) / (HEADS * HEAD_DIM) + EPSILON)
        mbuf[...] = jnp.broadcast_to(inverse, (ROWS, 128))

        @pl.loop(0, CHIPS)
        def _(h):
            lk[:, cols(h)] = (mixed[:, cols(h)] * mbuf[...] * gain[:, cols(h)]).astype(BF16)

        store.start()

    @pl.loop(0, CHIPS // 2)
    def _(i):
        pair = pair_from(i)
        base = pair * (pair + 1) // 2
        sbuf[0:2, :, 0:128] = jnp.zeros((2, ROWS, HEAD_DIM), F32)

        @pl.loop(0, pair + 1)
        def _(t):
            values = vbuf[pl.ds(t * 4, 4)].reshape(CHUNK, HEAD_DIM)
            for n in range(2):
                sbuf[n, :, 0:128] += jnp.dot(pbuf[base + t, n * 256:(n + 1) * 256], values, preferred_element_type=F32)

        for half in range(2):
            b = 2 * pair + half
            s = position(b)
            qbuf[b] = (sbuf[half, :, 0:128] / jnp.sum(lbuf[b], axis=1, keepdims=True)).astype(BF16)

            @pl.when(s == me)
            def _():
                pltpu.make_async_copy(qbuf.at[b], soft_out.at[:, cols(chip)], o_recv.at[chip]).start()

            @pl.when(s != me)
            def _():
                remote(qbuf.at[b], soft_out.at[:, cols(chip)], o_send.at[b], o_recv.at[chip], s).start()

        pl.when(i == 1)(carry)
        pl.when(i == 4)(normalize)

    sent(kbuf, soft_k, k_send, k_fwd)
    sent(vbuf, soft_v, v_send, v_fwd)

    @pl.when(q_core != core)
    def _():
        remote(soft_q.at[:, cols(0)], qbuf.at[0], q_send.at[0], q_send.at[0], partner).wait_send()

    @pl.loop(1, CHIPS)
    def _(i):
        remote(soft_q.at[:, cols(0)], qbuf.at[0], q_send.at[i], q_send.at[i], partner).wait_send()
        remote(chip_half.at[0], chip_half.at[0], one_send.at[i], one_send.at[i], partner).wait_send()
        remote(chip_half.at[0], chip_half.at[0], two_send.at[i], two_send.at[i], partner).wait_send()

    @pl.loop(0, CHIPS)
    def _(b):
        @pl.when(position(b) != me)
        def _():
            remote(qbuf.at[0], qbuf.at[0], o_send.at[b], o_send.at[b], partner).wait_send()

        arrived(soft_out.at[:, cols(b)], o_recv.at[b])

    store.wait()


def shards(lin_q, lin_k, lin_v, lin_gain, soft_q, soft_k, soft_v):
    half = pltpu.VMEM((CHIPS, 64, HEAD_DIM), F32)
    tokens = pltpu.VMEM((ROWS, CHIPS * HEAD_DIM), BF16)
    dma = pltpu.SemaphoreType.DMA
    hbm = pl.BlockSpec(memory_space=pl.ANY)
    shape = jax.ShapeDtypeStruct(lin_q.shape, BF16)
    return pl.pallas_call(
        kernel,
        out_shape=(shape, shape),
        in_specs=[hbm, hbm, hbm, pl.BlockSpec(memory_space=pltpu.VMEM), hbm, hbm, hbm],
        out_specs=(hbm, hbm),
        scratch_shapes=[
            tokens, tokens, tokens,
            pltpu.VMEM((ROWS, CHIPS * HEAD_DIM), F32),
            pltpu.VMEM((CHIPS, HEAD_DIM, HEAD_DIM), F32),
            half, half, half, half, half, half,
            pltpu.VMEM((4, ROWS, 128), F32),
            pltpu.VMEM((2 * CHIPS, ROWS, HEAD_DIM), BF16),
            pltpu.VMEM((2 * CHIPS, ROWS, HEAD_DIM), BF16),
            pltpu.VMEM((CHIPS, ROWS, HEAD_DIM), BF16),
            pltpu.VMEM((SEQ // CHUNK + 1, ROWS, CHUNK), F32),
            pltpu.VMEM((36, 2 * ROWS, CHUNK), BF16),
            pltpu.VMEM((CHIPS, ROWS, 128), F32),
            pltpu.VMEM((ROWS, 128), F32),
            dma((4,)),
            dma((CHIPS,)), dma((2 * CHIPS,)), dma((CHIPS,)),
            dma((CHIPS,)), dma((2 * CHIPS,)), dma((CHIPS,)),
            dma((CHIPS,)), dma((CHIPS,)),
            dma((CHIPS,)), dma((CHIPS,)),
            dma((4,)),
            dma((CHIPS,)), dma((CHIPS,)),
            dma((CHIPS,)), dma((CHIPS,)),
            dma((4,)), dma((4,)),
        ],
        compiler_params=pltpu.CompilerParams(
            collective_id=0, has_side_effects=True, vmem_limit_bytes=67043328),
    )(lin_q, lin_k, lin_v, lin_gain.reshape(1, -1), soft_q, soft_k, soft_v)


def solution(mesh):
    split = P("seq", "grp")
    return jax.shard_map(
        shards,
        mesh=mesh,
        in_specs=(split, split, split, P("grp"), split, split, split),
        out_specs=(split, split),
        check_vma=False,
    )
```
